32 devices in a mesh: section: 2 (over core), rep: 4 (over y, x), shard: 4 (over z).
Axes of the slice: x: 2, y: 2, z: 4, core: 2. Of those that a mesh axis runs over, the one named last changes fastest.
Arguments:
- tokens: bfloat16 [4096, 2048], P(('rep', 'shard')), may hold values from -6 to 6
- cotangent: bfloat16 [4096, 2048], P(('rep', 'shard')), may hold values from -6 to 6
- lengths: int32 [16, 2, 3], P(('rep', 'shard')), may hold values from 1 to 64, 128 in all within a row
- qkv_weight: bfloat16 [2, 2048, 6144], P('section', 'shard'), may hold values from -0.125 to 0.125
- qkv_bias: bfloat16 [2, 6144], P('section', 'shard'), may hold values from -3 to 3
- out_weight: bfloat16 [2, 2048, 2048], P('section', 'shard'), may hold values from -0.5 to 0.5
- out_bias: bfloat16 [2, 2048], P('section', 'shard'), may hold values from -3 to 3
- up_weight: bfloat16 [2, 2048, 8192], P('section', 'shard'), may hold values from -0.125 to 0.125
- up_bias: bfloat16 [2, 8192], P('section', 'shard'), may hold values from -3 to 3
- down_weight: bfloat16 [2, 8192, 2048], P('section', 'shard'), may hold values from -0.0625 to 0.0625
- down_bias: bfloat16 [2, 2048], P('section', 'shard'), may hold values from -3 to 3
- norm_gain: bfloat16 [2, 2048], P('section', 'shard'), may hold values from 0.5 to 1.5
- norm_bias: bfloat16 [2, 2048], P('section', 'shard'), may hold values from -2 to 2
Outputs:
- layer_outputs: bfloat16 [2, 4096, 2048], P('section', ('rep', 'shard'))
- input_grads: bfloat16 [2, 4096, 2048], P('section', ('rep', 'shard'))
- grad_qkv_weight: float32 [2, 2048, 6144], P('section', 'shard')
- grad_qkv_bias: float32 [2, 6144], P('section', 'shard')
- grad_out_weight: float32 [2, 2048, 2048], P('section', 'shard')
- grad_out_bias: float32 [2, 2048], P('section', 'shard')
- grad_up_weight: float32 [2, 2048, 8192], P('section', 'shard')
- grad_up_bias: float32 [2, 8192], P('section', 'shard')
- grad_down_weight: float32 [2, 8192, 2048], P('section', 'shard')
- grad_down_bias: float32 [2, 2048], P('section', 'shard')
- grad_norm_gain: float32 [2, 2048], P('section', 'shard')
- grad_norm_bias: float32 [2, 2048], P('section', 'shard')
The draws below stay inside these ranges and needn't reach their ends.
Inputs may be any that keep to these rules, and one draw needn't show every extreme that they name: The 3 lengths of every block sum to 128, and in every block the longest is exactly 64.
All inputs are finite; a program needn't handle non-finite values.
Results may differ from the reference program's by a relative error of at most 0.017.
Values may be sent and summed in bfloat16 or wider, within the bound.
No kernel may reach another device: no remote copies, remote signals or barrier semaphores. Data moves between devices by JAX's collectives and lax.ppermute only.
A program may use at most 512 MiB of HBM per device.

```python
import math
import jax
import jax.numpy as jnp
import numpy as np
from jax import lax

D = 2048
HEADS = 32
HEAD_DIM = 64
ROTARY = 32
FF = 8192
MICRO_TOK = 128
MICRO_BATCHES = 2
SEGMENTS = 3
LAYERS = 2
SEQ_MAX = 64
DATA_DEV = 16
TOKENS = 4096


def spiked(drawn, own_key, source, target, blocks, factor):
    def block_of(axis_at):
        return (jnp.arange(drawn.shape[axis_at]) // (drawn.shape[axis_at] // blocks)).reshape((-1,) + (1,) * (drawn.ndim - 1 - axis_at))

    one_side = jax.random.permutation(own_key, blocks)[block_of(target)]
    second = (block_of(target) + blocks // 2) % blocks
    return jnp.where((block_of(source) == one_side) | (block_of(source) == second), factor * drawn, drawn)


def steps_of(rng, shape, pieces, least, high):
    gain = 1.0
    for axis_at, blocks in pieces:
        steps = jax.random.uniform(jax.random.fold_in(jax.random.fold_in(rng, 6), axis_at), (blocks,), jnp.float32, least / len(pieces), high / len(pieces))
        gain = gain * jnp.repeat(jnp.exp(steps), shape[axis_at] // blocks).reshape((-1,) + (1,) * (len(shape) - 1 - axis_at))
    return gain


def split_up(count, total, bound, skew):
    loads = [(1 << 20) // math.isqrt(standing ** skew) + 1 for standing in range(2, count + 1)]
    rest, holding = total - bound - (count - 1), [1] * (count - 1)
    while rest > 0:
        free = [i for i in range(count - 1) if holding[i] < bound]
        whole, remaining = sum([loads[i] for i in free]), rest
        for i in free:
            more = min(bound - holding[i], max(1, remaining * loads[i] // whole), rest)
            holding[i] = holding[i] + more
            rest = rest - more
    return np.array([bound] + holding)


def uneven_parts(rng, amount, total, most, skew):
    if amount == 2:
        one = jax.random.randint(rng, (), max(1, total - most), min(most, total - 1) + 1)
        return jnp.stack([one, total - one])
    sizes = jnp.asarray(split_up(amount, total, most, skew), jnp.int32)
    pairs = (amount - 1) // 2
    donor, taker = sizes[1:1 + 2 * pairs:2], sizes[2:2 + 2 * pairs:2]
    margin = jnp.minimum(donor - 1, most - taker)
    moved = jax.random.randint(jax.random.fold_in(rng, 1), (pairs,), 0, 1 << 20) % (margin + 1)
    sizes = sizes.at[1:1 + 2 * pairs:2].set(donor - moved).at[2:2 + 2 * pairs:2].set(taker + moved)
    return sizes[jax.random.permutation(jax.random.fold_in(rng, 2), amount)]


def scatter_about(key, dims, width, bound, shards=(), kind=jnp.bfloat16):
    loudness = steps_of(key, dims, shards, -0.22, 0.18) if shards else 1.0
    values = jax.random.normal(key, dims, jnp.float32) * width * loudness
    return jnp.minimum(jnp.maximum(values, -bound), bound).astype(kind)


def bell_draw_with(key, shape, scale, reach, split, heavy, kind=jnp.bfloat16):
    entries = scale * jax.random.normal(key, shape, jnp.float32)
    if split:
        entries = entries * steps_of(key, shape, split, -0.22, 0.18)
    return jnp.clip(spiked(entries, jax.random.fold_in(key, 3), *heavy), -reach, reach).astype(kind)


def setup_inputs(seed: int = 0) -> dict:
    key_list = jax.random.split(jax.random.key(seed), 14)
    tokens = bell_draw_with(key_list[0], (TOKENS, D), 1.0, 6.0, ((0, 16),), (0, 1, 16, 2.0))
    cotangent = scatter_about(key_list[1], (TOKENS, D), 1.0, 6.0, ((0, 16),))
    lengths = jax.vmap(lambda own: uneven_parts(own, SEGMENTS, MICRO_TOK, SEQ_MAX, 2))(jax.random.split(key_list[2], DATA_DEV * MICRO_BATCHES)).reshape((DATA_DEV, MICRO_BATCHES, SEGMENTS)).astype(jnp.int32)
    qkv_weight = scatter_about(key_list[3], (LAYERS, D, 3 * D), D ** -0.5, 0.125, ((0, 2), (1, 4)))
    qkv_bias = scatter_about(key_list[4], (LAYERS, 3 * D), 0.5, 3.0, ((0, 2), (1, 4)))
    out_weight = scatter_about(key_list[5], (LAYERS, D, D), (D // 16) ** -0.5, 0.5, ((0, 2), (1, 4)))
    out_bias = scatter_about(key_list[6], (LAYERS, D), 0.5, 3.0, ((0, 2), (1, 4)))
    up_weight = scatter_about(key_list[7], (LAYERS, D, FF), D ** -0.5, 0.125, ((0, 2), (1, 4)))
    up_bias = scatter_about(key_list[8], (LAYERS, FF), 0.5, 3.0, ((0, 2), (1, 4)))
    down_weight = scatter_about(key_list[9], (LAYERS, FF, D), FF ** -0.5, 0.0625, ((0, 2), (1, 4)))
    down_bias = scatter_about(key_list[10], (LAYERS, D), 0.5, 3.0, ((0, 2), (1, 4)))
    norm_gain = jnp.clip(1.0 + 0.1 * jax.random.normal(key_list[11], (LAYERS, D), jnp.float32), 0.5, 1.5).astype(jnp.bfloat16)
    norm_bias = scatter_about(key_list[12], (LAYERS, D), 0.3, 2.0, ((0, 2), (1, 4)))
    return {"tokens": tokens, "cotangent": cotangent, "lengths": lengths, "qkv_weight": qkv_weight, "qkv_bias": qkv_bias, "out_weight": out_weight, "out_bias": out_bias, "up_weight": up_weight, "up_bias": up_bias, "down_weight": down_weight, "down_bias": down_bias, "norm_gain": norm_gain, "norm_bias": norm_bias}


@jax.custom_vjp
def low(v):
    return lax.optimization_barrier(v.astype(jnp.bfloat16)).astype(jnp.float32)

@jax.custom_vjp
def low_back(v):
    return v

def low_keep(v):
    return (low(v), None)

def low_pass(kept, grad):
    return (grad,)

def back_keep(v):
    return (v, None)

def back_low(kept, grad):
    return (low(grad),)
low.defvjp(low_keep, low_pass)
low_back.defvjp(back_keep, back_low)
masked_score = -1e+30
norm_epsilon = 1e-05
rotary_base = 10000.0

def segment_layout(seq_lengths, block_rows):
    places = jnp.arange(block_rows, dtype=jnp.int32)
    seq_ends = jnp.cumsum(seq_lengths).astype(jnp.int32)
    seq_starts = (seq_ends - seq_lengths).astype(jnp.int32)
    member = lax.optimization_barrier(jnp.sum((places[:, None] >= seq_ends[None, :]).astype(jnp.int32), axis=1)).astype(jnp.int32)
    picked = member[:, None] == jnp.arange(seq_lengths.shape[0], dtype=jnp.int32)[None, :]
    begins = lax.optimization_barrier(jnp.sum(jnp.where(picked, seq_starts[None, :], 0), axis=1)).astype(jnp.int32)
    offsets = (places - begins).astype(jnp.float32)
    allowed = (member[:, None] == member[None, :]) & (places[None, :] <= places[:, None])
    return (offsets, allowed)

def rotary_tables(offsets, rotary_dims):
    half_dims = rotary_dims // 2
    exponent = jnp.arange(half_dims, dtype=jnp.float32) * (2.0 / rotary_dims)
    frequency = jnp.power(rotary_base, -exponent)
    angles = offsets[:, None] * frequency[None, :]
    cosine = jnp.cos(angles)
    sine_part = jnp.sin(angles)
    return (jnp.concatenate([cosine, cosine], axis=1), jnp.concatenate([sine_part, sine_part], axis=1))

def apply_rotary(head_values, cosine_table, sine_table):
    rotary_dims = cosine_table.shape[1]
    half_dims = rotary_dims // 2
    turned = head_values[..., :rotary_dims]
    swapped = jnp.concatenate([-turned[..., half_dims:], turned[..., :half_dims]], axis=-1)
    turned = turned * cosine_table[:, None, :] + swapped * sine_table[:, None, :]
    return jnp.concatenate([turned, head_values[..., rotary_dims:]], axis=-1)

def normalize(inputs, gain_row, bias_row):
    centered = inputs - lax.optimization_barrier(jnp.mean(inputs, axis=1, keepdims=True))
    variance = lax.optimization_barrier(jnp.mean(centered * centered, axis=1, keepdims=True))
    return centered * lax.rsqrt(variance + norm_epsilon) * gain_row + bias_row

def gelu_tanh(values):
    return jax.nn.gelu(values, approximate=True)

def block_attention(paired):
    mixed_block, seq_lengths = paired
    row_count = mixed_block.shape[0]
    offsets, allowed = segment_layout(seq_lengths, row_count)
    cosine_table, sine_table = rotary_tables(offsets, ROTARY)
    grouped = mixed_block.reshape(row_count, 3, HEADS, HEAD_DIM)
    queries = low(apply_rotary(grouped[:, 0], cosine_table, sine_table))
    keys = low(apply_rotary(grouped[:, 1], cosine_table, sine_table))
    values = low(grouped[:, 2])
    scores = jnp.einsum('qhd,khd->hqk', queries, keys, precision=lax.Precision.HIGHEST)
    scores = low_back(scores * HEAD_DIM ** (-0.5))
    scores = jnp.where(allowed[None], scores, masked_score)
    probs = low(jax.nn.softmax(scores, axis=2))
    context = jnp.einsum('hqk,khd->qhd', probs, values, precision=lax.Precision.HIGHEST)
    return context.reshape(row_count, HEADS * HEAD_DIM)

def layer(inputs, params, seq_table):
    qkv_matrix, qkv_shift, out_matrix, out_shift, up_matrix, up_shift, down_matrix, down_shift, gain_vector, bias_vector = params
    normed = low(normalize(inputs, gain_vector, bias_vector))
    mixed = low_back(jnp.dot(normed, qkv_matrix, precision=lax.Precision.HIGHEST) + qkv_shift)
    hidden = low_back(jnp.dot(normed, up_matrix, precision=lax.Precision.HIGHEST) + up_shift)
    activated = low(gelu_tanh(hidden))
    block_count = seq_table.shape[0]
    blocks = mixed.reshape(block_count, -1, mixed.shape[1])
    context = lax.map(jax.checkpoint(block_attention), (blocks, seq_table))
    context = low(low_back(context.reshape(inputs.shape[0], -1)))
    attention_out = jnp.dot(context, out_matrix, precision=lax.Precision.HIGHEST) + out_shift
    mlp_out = jnp.dot(activated, down_matrix, precision=lax.Precision.HIGHEST) + down_shift
    return inputs + attention_out + mlp_out

def reference(tokens, cotangent, lengths, qkv_weight, qkv_bias, out_weight, out_bias, up_weight, up_bias, down_weight, down_bias, norm_gain, norm_bias):
    seq_table = lengths.reshape(-1, lengths.shape[-1]).astype(jnp.int32)
    params = tuple((member_array.astype(jnp.float32) for member_array in (qkv_weight, qkv_bias, out_weight, out_bias, up_weight, up_bias, down_weight, down_bias, norm_gain, norm_bias)))
    start_rows = tokens.astype(jnp.float32)
    layer_count = qkv_weight.shape[0]
    probes = jnp.zeros((layer_count,) + start_rows.shape, jnp.float32)

    def whole(probe_rows, layer_params):
        current = start_rows
        outputs = []
        for layer_id in range(layer_count):
            if layer_id > 0:
                current = low_back(low(current))
            current = current + probe_rows[layer_id]
            current = layer(current, tuple((member_array[layer_id] for member_array in layer_params)), seq_table)
            outputs.append(current)
        return (current, jnp.stack(outputs))
    last_rows, back_fn, stacked = jax.vjp(whole, probes, params, has_aux=True)
    grad_probes, grad_params = back_fn(cotangent.astype(jnp.float32))
    return (stacked.astype(jnp.bfloat16), grad_probes.astype(jnp.bfloat16), grad_params[0], grad_params[1], grad_params[2], grad_params[3], grad_params[4], grad_params[5], grad_params[6], grad_params[7], grad_params[8], grad_params[9])
```

```python
import functools

import jax
import jax.numpy as jnp
from jax import lax
from jax.sharding import PartitionSpec as P

HEADS = 32
HEAD_DIM = 64
ROTARY = 32
MICRO_BATCHES = 2
LAYERS = 2


masked_score = -1e30
norm_epsilon = 1e-05
rotary_base = 10000.0


low = jnp.bfloat16
wide = jnp.float32


def segment_layout(seq_lengths, block_rows):
    places = jnp.arange(block_rows, dtype=jnp.int32)
    seq_ends = jnp.cumsum(seq_lengths)
    seq_starts = seq_ends - seq_lengths
    member = jnp.sum((places[:, None] >= seq_ends[None, :]).astype(jnp.int32), axis=1)
    picked = member[:, None] == jnp.arange(seq_lengths.shape[0], dtype=jnp.int32)[None, :]
    begins = jnp.sum(jnp.where(picked, seq_starts[None, :], 0), axis=1)
    offsets = (places - begins).astype(jnp.float32)
    allowed = (member[:, None] == member[None, :]) & (places[None, :] <= places[:, None])
    return (offsets, allowed)


def rotary_tables(offsets, rotary_dims):
    half_dims = rotary_dims // 2
    exponent = jnp.arange(half_dims, dtype=jnp.float32) * (2.0 / rotary_dims)
    frequency = jnp.power(rotary_base, -exponent)
    angles = offsets[:, None] * frequency[None, :]
    cosine = jnp.cos(angles)
    sine_part = jnp.sin(angles)
    return (
        jnp.concatenate([cosine, cosine], axis=1),
        jnp.concatenate([sine_part, sine_part], axis=1),
    )


def apply_rotary(head_values, cosine_table, sine_table):
    rotary_dims = cosine_table.shape[1]
    half_dims = rotary_dims // 2
    turned = head_values[..., :rotary_dims]
    swapped = jnp.concatenate([-turned[..., half_dims:], turned[..., :half_dims]], axis=-1)
    turned = turned * cosine_table[:, None, :] + swapped * sine_table[:, None, :]
    return jnp.concatenate([turned, head_values[..., rotary_dims:]], axis=-1)


def unapply_rotary(grads, cosine_table, sine_table):
    rotary_dims = cosine_table.shape[1]
    half_dims = rotary_dims // 2
    turned = grads[..., :rotary_dims]
    scaled = turned * sine_table[:, None, :]
    swapped = jnp.concatenate([scaled[..., half_dims:], -scaled[..., :half_dims]], axis=-1)
    turned = turned * cosine_table[:, None, :] + swapped
    return jnp.concatenate([turned, grads[..., rotary_dims:]], axis=-1)


def normalize(inputs, gain_row, bias_row):
    centered = inputs - jnp.mean(inputs, axis=1, keepdims=True)
    variance = jnp.mean(centered * centered, axis=1, keepdims=True)
    return centered * lax.rsqrt(variance + norm_epsilon) * gain_row + bias_row


def gelu_tanh(values):
    return jax.nn.gelu(values, approximate=True)


def times(left, right):
    return lax.dot_general(left, right, (((1,), (0,)), ((), ())), preferred_element_type=wide)


def times_transposed(left, right):
    return lax.dot_general(left, right, (((1,), (1,)), ((), ())), preferred_element_type=wide)


def transposed_times(left, right):
    return lax.dot_general(left, right, (((0,), (0,)), ((), ())), preferred_element_type=wide)


def masked_scores(queries, keys, allowed):
    scores = jnp.einsum("bqhd,bkhd->bhqk", queries, keys, preferred_element_type=wide)
    scores = scores * queries.shape[-1] ** (-0.5)
    return jnp.where(allowed[:, None], scores, masked_score)


def attend(queries, keys, values, allowed):
    scores = masked_scores(queries, keys, allowed)
    peak = jnp.max(scores, axis=3, keepdims=True)
    expon = jnp.exp(scores - peak)
    totals = jnp.sum(expon, axis=3, keepdims=True)
    probs = (expon / totals).astype(low)
    context = jnp.einsum("bhqk,bkhd->bqhd", probs, values, preferred_element_type=wide)
    return (context, peak + jnp.log(totals))


def attend_back(queries, keys, values, allowed, log_total, grad_context):
    scale_factor = queries.shape[-1] ** (-0.5)
    probs = jnp.exp(masked_scores(queries, keys, allowed) - log_total)
    grad_probs = jnp.einsum("bqhd,bkhd->bhqk", grad_context, values, preferred_element_type=wide)
    grad_values = jnp.einsum(
        "bhqk,bqhd->bkhd", probs.astype(low), grad_context, preferred_element_type=wide
    )
    inner = jnp.sum(grad_probs * probs, axis=3, keepdims=True)
    grad_scores = (probs * (grad_probs - inner)).astype(low)
    grad_queries = (
        jnp.einsum("bhqk,bkhd->bqhd", grad_scores, keys, preferred_element_type=wide) * scale_factor
    )
    grad_keys = (
        jnp.einsum("bhqk,bqhd->bkhd", grad_scores, queries, preferred_element_type=wide)
        * scale_factor
    )
    return (grad_queries, grad_keys, grad_values)


def swap_cores(array):
    return lax.ppermute(array, "section", [(0, 1), (1, 0)])


def shifted(array, by):
    count = lax.axis_size("shard")
    return lax.ppermute(array, "shard", [(i, (i + by) % count) for i in range(count)])


def gather_rows(own):
    count = lax.axis_size("shard")
    mine = [own] + [shifted(own, k) for k in range(1, count)]
    other = [swap_cores(block) for block in mine]
    return jnp.concatenate(mine + other, axis=0)


def reduce_rows(partial):
    count = lax.axis_size("shard")
    half = partial.shape[0] // 2
    block = half // count
    total = None
    for k in range(count):
        mine = partial[k * block : (k + 1) * block]
        other = partial[half + k * block : half + (k + 1) * block].astype(low)
        merged = mine + swap_cores(other).astype(wide)
        if k > 0:
            merged = shifted(merged.astype(low), -k).astype(wide)
        total = merged if total is None else total + merged
    return total


def on_device(
    tokens,
    cotangent,
    lengths,
    qkv_weight,
    qkv_bias,
    out_weight,
    out_bias,
    up_weight,
    up_bias,
    down_weight,
    down_bias,
    norm_gain,
    norm_bias,
):
    cores = lax.axis_size("section")
    reps = lax.axis_size("rep")
    shards = lax.axis_size("shard")
    core = lax.axis_index("section")
    rep = lax.axis_index("rep")
    shard = lax.axis_index("shard")
    first = core == 0
    block_rows = tokens.shape[0] // MICRO_BATCHES
    model = tokens.shape[1]
    ff = up_weight.shape[2]
    in_rows = qkv_weight.shape[1]
    piece = in_rows // reps
    head_cols = model // (shards * cores)
    ff_cols = ff // (shards * cores)
    heads = head_cols // HEAD_DIM
    mixed_cols = 3 * head_cols
    blocks = cores * shards
    own_tokens = lax.dynamic_slice_in_dim(tokens, core * block_rows, block_rows, 0)
    own_grad = lax.dynamic_slice_in_dim(cotangent, core * block_rows, block_rows, 0)

    def both_layers(halves):
        kept = lax.dynamic_index_in_dim(halves, core, 0, False)
        sent = lax.dynamic_index_in_dim(halves, 1 - core, 0, False)
        came = swap_cores(sent)
        return (jnp.where(first, kept, came), jnp.where(first, came, kept))

    widths = [qkv_bias.shape[1], in_rows, up_bias.shape[1], in_rows, in_rows, in_rows]
    packed = jnp.concatenate(
        [
            qkv_bias[0],
            out_bias[0],
            up_bias[0],
            down_bias[0],
            norm_gain[0],
            norm_bias[0],
            lengths.reshape(-1).astype(low),
        ]
    )
    small = lax.all_gather(packed, ("section", "shard"), axis=0, tiled=False)
    small = small.reshape(cores, shards, -1)
    starts = [sum(widths[:i]) for i in range(len(widths) + 1)]

    def vectors(layer):
        cut = [small[layer, :, starts[i] : starts[i + 1]].astype(wide) for i in range(len(widths))]
        qkv = cut[0].reshape(3, shards, cores, head_cols)
        qkv = lax.dynamic_index_in_dim(qkv, shard, 1, False)
        qkv = lax.dynamic_index_in_dim(qkv, core, 1, False).reshape(-1)
        up = lax.dynamic_index_in_dim(cut[2], shard, 0, False).reshape(cores, ff_cols)
        up = lax.dynamic_index_in_dim(up, core, 0, False)
        return (
            jnp.concatenate([qkv, up]),
            (cut[1] + cut[3]).reshape(-1),
            cut[4].reshape(-1),
            cut[5].reshape(-1),
        )

    table = small[0, :, starts[-1] :].reshape(shards, MICRO_BATCHES, -1).astype(jnp.int32)
    back = table[::-1]
    turned = lax.dynamic_slice_in_dim(
        jnp.concatenate([back, back], axis=0), shards - 1 - shard, shards, 0
    )
    mine = lax.dynamic_index_in_dim(turned, core, 1, False)
    others = lax.dynamic_index_in_dim(turned, 1 - core, 1, False)
    seq_table = jnp.concatenate([mine, others], axis=0)
    offsets, allowed = jax.vmap(lambda row: segment_layout(row, block_rows))(seq_table)
    cosine_table, sine_table = rotary_tables(offsets.reshape(-1), ROTARY)

    qkv_rows = lax.dynamic_slice_in_dim(qkv_weight[0], rep * piece, piece, 0)
    up_rows = lax.dynamic_slice_in_dim(up_weight[0], rep * piece, piece, 0)
    qkv_rows = qkv_rows.reshape(piece, 3, shards, cores, head_cols).transpose(3, 2, 0, 1, 4)
    up_rows = up_rows.reshape(piece, shards, cores, ff_cols).transpose(2, 1, 0, 3)
    in_halves = jnp.concatenate(
        [qkv_rows.reshape(cores, shards, piece, mixed_cols), up_rows], axis=3
    )
    in_parts = both_layers(in_halves)

    def columns_of(part):
        turned_part = lax.all_to_all(part, "shard", split_axis=0, concat_axis=0, tiled=True)
        whole = lax.all_gather(turned_part, "rep", axis=0, tiled=False)
        return whole.reshape(model, mixed_cols + ff_cols)

    in_weights = [columns_of(part) for part in in_parts]
    down_halves = down_weight[0].reshape(cores, reps, ff_cols // reps, model)
    out_halves = out_weight[0].reshape(cores, reps, head_cols // reps, model)
    out_parts = both_layers(jnp.concatenate([down_halves, out_halves], axis=2))
    down_piece = ff_cols // reps
    out_piece = head_cols // reps
    out_weights = [part.reshape(-1, model) for part in out_parts]

    def join(down_side, out_side):
        count = down_side.shape[0]
        return jnp.concatenate(
            [
                down_side.reshape(count, reps, down_piece),
                out_side.reshape(count, reps, out_piece),
            ],
            axis=2,
        ).reshape(count, -1)

    def split(joined):
        count = joined.shape[0]
        parts = joined.reshape(count, reps, down_piece + out_piece)
        return (
            parts[:, :, :down_piece].reshape(count, -1),
            parts[:, :, down_piece:].reshape(count, -1),
        )

    def permuted(rows):
        count = rows.shape[0]
        return rows.reshape(count, shards, reps, piece).transpose(0, 2, 1, 3).reshape(count, -1)

    def unpermuted(rows):
        count = rows.shape[0]
        return rows.reshape(count, reps, shards, piece).transpose(0, 2, 1, 3).reshape(count, -1)

    own_vectors = [vectors(layer) for layer in range(LAYERS)]
    state = []
    inputs = own_tokens
    results = []
    for layer in range(LAYERS):
        in_shift, out_shift, gain, shift = own_vectors[layer]
        normed = normalize(inputs.astype(wide), gain, shift).astype(low)
        normed = gather_rows(permuted(normed))
        joined = times(normed, in_weights[layer]) + in_shift
        count = normed.shape[0]
        grouped = joined[:, :mixed_cols].reshape(count, 3, heads, HEAD_DIM)
        hidden = joined[:, mixed_cols:]
        by_block = (blocks, block_rows, heads, HEAD_DIM)
        queries = apply_rotary(grouped[:, 0], cosine_table, sine_table).astype(low)
        keys = apply_rotary(grouped[:, 1], cosine_table, sine_table).astype(low)
        values = grouped[:, 2].astype(low)
        queries, keys, values = (part.reshape(by_block) for part in (queries, keys, values))
        context, log_total = attend(queries, keys, values, allowed)
        context = context.astype(low).reshape(count, head_cols)
        activated = gelu_tanh(hidden).astype(low)
        before_out = join(activated, context)
        partial = times(before_out, out_weights[layer])
        result = inputs.astype(wide) + reduce_rows(partial) + out_shift
        result = result.astype(low)
        state.append((inputs, normed, queries, keys, values, log_total, hidden, before_out))
        results.append(result)
        inputs = result

    grad = own_grad
    input_grads = [None] * LAYERS
    big = [None] * LAYERS
    sums = [None] * LAYERS
    for layer in reversed(range(LAYERS)):
        in_shift, out_shift, gain, shift = own_vectors[layer]
        inputs, normed, queries, keys, values, log_total, hidden, before_out = state[layer]
        grad_rows = gather_rows(grad)
        count = grad_rows.shape[0]
        grad_before = times_transposed(grad_rows, out_weights[layer])
        grad_active, grad_context = split(grad_before)
        grad_context = grad_context.astype(low).reshape(queries.shape)
        unused_out, gelu_back = jax.vjp(gelu_tanh, hidden)
        grad_hidden = gelu_back(grad_active)[0].astype(low)
        three = attend_back(queries, keys, values, allowed, log_total, grad_context)
        grad_queries, grad_keys, grad_values = (
            part.reshape(count, heads, HEAD_DIM) for part in three
        )
        grad_queries = unapply_rotary(grad_queries, cosine_table, sine_table)
        grad_keys = unapply_rotary(grad_keys, cosine_table, sine_table)
        grad_mixed = (
            jnp.stack([grad_queries, grad_keys, grad_values], axis=1)
            .reshape(count, -1)
            .astype(low)
        )
        grad_joined = jnp.concatenate([grad_mixed, grad_hidden], axis=1)
        grad_normed = unpermuted(reduce_rows(times_transposed(grad_joined, in_weights[layer])))
        unused_out, norm_back = jax.vjp(normalize, inputs.astype(wide), gain, shift)
        grad_inputs, grad_gain, grad_bias = norm_back(grad_normed)
        sums[layer] = (
            jnp.sum(grad_joined, axis=0, dtype=wide),
            jnp.sum(grad.astype(wide), axis=0),
            grad_gain,
            grad_bias,
        )
        out_grad = transposed_times(before_out, grad_rows).astype(low)
        in_grad = transposed_times(normed, grad_joined).astype(low)
        out_own = lax.psum_scatter(out_grad, "rep", scatter_dimension=0, tiled=True)
        in_own = lax.psum_scatter(in_grad, "rep", scatter_dimension=0, tiled=True)
        in_own = lax.all_to_all(
            in_own.reshape(shards, piece, -1), "shard", split_axis=0, concat_axis=0, tiled=True
        )
        big[layer] = (
            lax.all_gather(out_own, ("section", "rep"), axis=0, tiled=False),
            lax.all_gather(in_own, ("section", "rep"), axis=0, tiled=False),
        )
        grad = (grad.astype(wide) + grad_inputs).astype(low)
        input_grads[layer] = grad

    rows = []
    for layer in range(LAYERS):
        joined_sum, out_sum, gain_sum, bias_sum = sums[layer]
        qkv_slot = jnp.zeros((3, shards, cores, head_cols), wide)
        qkv_slot = lax.dynamic_update_slice(
            qkv_slot, joined_sum[:mixed_cols].reshape(3, 1, 1, head_cols), (0, shard, core, 0)
        )
        up_slot = jnp.zeros((shards, cores, ff_cols), wide)
        up_slot = lax.dynamic_update_slice(
            up_slot, joined_sum[mixed_cols:].reshape(1, 1, ff_cols), (shard, core, 0)
        )
        rows.append(
            jnp.concatenate([qkv_slot.reshape(-1), out_sum, up_slot.reshape(-1), gain_sum, bias_sum])
        )
    summed = lax.psum(jnp.stack(rows), ("section", "rep", "shard"))
    summed = lax.dynamic_index_in_dim(summed, core, 0, False)
    lens = [3 * model, model, ff, model, model]
    at = [sum(lens[:i]) for i in range(len(lens) + 1)]

    def own_part(index):
        cut = summed[at[index] : at[index + 1]].reshape(shards, -1)
        return lax.dynamic_index_in_dim(cut, shard, 0, True)

    qkv_b, out_b, up_b, gain_g, bias_g = (own_part(i) for i in range(5))

    out_all = jnp.where(first, big[0][0], big[1][0])
    out_all = out_all.reshape(cores, reps, down_piece + out_piece, model)
    grad_down = out_all[:, :, :down_piece].reshape(1, -1, model).astype(wide)
    grad_out = out_all[:, :, down_piece:].reshape(1, -1, model).astype(wide)
    in_all = jnp.where(first, big[0][1], big[1][1])
    in_all = in_all.reshape(cores, reps, shards, piece, mixed_cols + ff_cols)
    grad_qkv = in_all[..., :mixed_cols].reshape(cores, reps, shards, piece, 3, head_cols)
    grad_qkv = grad_qkv.transpose(1, 3, 4, 2, 0, 5).reshape(1, in_rows, 3 * model).astype(wide)
    grad_up = in_all[..., mixed_cols:].transpose(1, 3, 2, 0, 4)
    grad_up = grad_up.reshape(1, in_rows, ff).astype(wide)

    def by_layer(pair):
        came = swap_cores(jnp.where(first, pair[1], pair[0]))
        own = jnp.where(first, pair[0], pair[1])
        low_rows = jnp.where(first, own, came)
        high_rows = jnp.where(first, came, own)
        return jnp.concatenate([low_rows, high_rows], axis=0)[None]

    return (
        by_layer(results),
        by_layer(input_grads),
        grad_qkv,
        qkv_b,
        grad_out,
        out_b,
        grad_up,
        up_b,
        grad_down,
        out_b,
        gain_g,
        bias_g,
    )


def solution(mesh):
    placed = (
        P(("rep", "shard"), None),
        P(("rep", "shard"), None),
        P(("rep", "shard"), None, None),
        P("section", "shard", None),
        P("section", "shard"),
        P("section", "shard", None),
        P("section", "shard"),
        P("section", "shard", None),
        P("section", "shard"),
        P("section", "shard", None),
        P("section", "shard"),
        P("section", "shard"),
        P("section", "shard"),
    )
    return jax.shard_map(
        on_device,
        mesh=mesh,
        in_specs=placed,
        out_specs=(
            P("section", ("rep", "shard"), None),
            P("section", ("rep", "shard"), None),
            P("section", "shard", None),
            P("section", "shard"),
            P("section", "shard", None),
            P("section", "shard"),
            P("section", "shard", None),
            P("section", "shard"),
            P("section", "shard", None),
            P("section", "shard"),
            P("section", "shard"),
            P("section", "shard"),
        ),
        check_vma=False,
    )
```
